256 devices in a mesh: rows: 4 (over z_hi, core), mp: 64 (over x, y, z_lo).
Axes of the slice: x: 4, y: 4, z: 8 (z_hi: 2, z_lo: 4; z = z_hi * 4 + z_lo), core: 2. Of those that a mesh axis runs over, the one named last changes fastest.
Arguments:
- inputs: bfloat16 [3, 512, 2304], P(None, 'rows', 'mp'), may hold values from -6 to 6
- gate_up: bfloat16 [3, 2304, 2, 9216], P(None, None, None, 'mp'), may hold values from -0.125 to 0.125
- down_weight: bfloat16 [3, 9216, 2304], P(None, 'mp'), may hold values from -0.1875 to 0.1875
- enc_weight: bfloat16 [3, 2304, 16384], P(None, None, 'mp'), may hold values from -0.125 to 0.125
- enc_bias: float32 [3, 16384], P(None, 'mp'), may hold values from -3 to 3
- dec_weight: bfloat16 [6, 16384, 2304], P(None, 'mp', 'rows'), may hold values from -0.1875 to 0.1875
Outputs:
- recon: float32 [3, 512, 2304], P(None, 'rows', 'mp')
- residual: float32 [3, 512, 2304], P(None, 'rows', 'mp')
The draws below stay inside these ranges and needn't reach their ends.
All inputs are finite; a program needn't handle non-finite values.
Results may differ from the reference program's by a relative error of at most 0.0029.
Values may be sent and summed in bfloat16 or wider, within the bound.
No kernel may reach another device: no remote copies, remote signals or barrier semaphores. Data moves between devices by JAX's collectives and lax.ppermute only.
A program may use at most 128 MiB of HBM per device.

```python
import jax
import jax.numpy as jnp

D = 2304
FF = 9216
LAT = 16384
LAYERS = 3
PAIRS = 6
TOKENS = 512


def strengthened(values, own_key, source, target, parts, factor):
    owner, partner = [(jnp.arange(values.shape[dim]) // (values.shape[dim] // parts)).reshape([-1 if axis == dim else 1 for axis in range(values.ndim)]) for dim in (source, target)]
    chosen = jax.random.permutation(own_key, parts)[partner]
    strong = (owner == chosen) | (owner == (partner + parts // 2) % parts)
    return jnp.where(strong, factor * values, values)


def block_scale(key, shape, shards, low, largest):
    factor_of = 1.0
    for position, shards_of in shards:
        steps = jax.random.uniform(jax.random.fold_in(jax.random.fold_in(key, 6), position), (shards_of,), jnp.float32, low / len(shards), largest / len(shards))
        factor_of = factor_of * jnp.repeat(jnp.exp(steps), shape[position] // shards_of).reshape((-1,) + (1,) * (len(shape) - 1 - position))
    return factor_of


def normal_values(rng, shape, width, reach, split=(), dtype=jnp.bfloat16):
    array = jax.random.normal(rng, shape, jnp.float32) * width
    if len(split) > 0:
        array = block_scale(rng, shape, split, -0.22, 0.18) * array
    return jnp.clip(array, min=-reach, max=reach).astype(dtype)


def gaussian_with(own_key, extent, deviation, reach, cuts, heavy, held_as=jnp.bfloat16):
    array = deviation * jax.random.normal(own_key, extent, jnp.float32)
    if cuts:
        array = array * block_scale(own_key, extent, cuts, -0.22, 0.18)
    return jnp.clip(strengthened(array, jax.random.fold_in(own_key, 3), *heavy), -reach, reach).astype(held_as)


def setup_inputs(seed: int = 0) -> dict:
    key_list = jax.random.split(jax.random.key(seed), 7)
    inputs = normal_values(key_list[0], (LAYERS, TOKENS, D), 1.0, 6.0, ((1, 4), (2, 64)))
    gate_up = normal_values(key_list[1], (LAYERS, D, 2, FF), D ** -0.5, 0.125, ((3, 64),))
    down_weight = gaussian_with(key_list[2], (LAYERS, FF, D), FF ** -0.5, 0.1875, ((1, 64),), (1, 2, 64, 4.0))
    enc_weight = normal_values(key_list[3], (LAYERS, D, LAT), D ** -0.5, 0.125, ((2, 64),))
    enc_bias = normal_values(key_list[4], (LAYERS, LAT), 0.5, 3.0, ((1, 64),), jnp.float32)
    dec_weight = gaussian_with(key_list[5], (PAIRS, LAT, D), (LAT // 2) ** -0.5, 0.1875, ((1, 64), (2, 4)), (1, 2, 64, 4.0))
    return {"inputs": inputs, "gate_up": gate_up, "down_weight": down_weight, "enc_weight": enc_weight, "enc_bias": enc_bias, "dec_weight": dec_weight}


def reference(inputs, gate_up, down_weight, enc_weight, enc_bias, dec_weight):
    targets = []
    latents = []
    for layer in range(LAYERS):
        rows_in = inputs[layer]
        gate = jnp.dot(rows_in, gate_up[layer, :, 0, :], preferred_element_type=jnp.float32)
        upper = jnp.dot(rows_in, gate_up[layer, :, 1, :], preferred_element_type=jnp.float32)
        hidden = (jax.nn.gelu(gate, approximate=True) * upper).astype(jnp.bfloat16)
        targets.append(jnp.dot(hidden, down_weight[layer], preferred_element_type=jnp.float32))
        pre_act = jnp.dot(rows_in, enc_weight[layer], preferred_element_type=jnp.float32) + enc_bias[layer][None, :]
        latents.append(jax.nn.relu(pre_act).astype(jnp.bfloat16))
    recons = []
    for target_layer in range(LAYERS):
        total = jnp.zeros((TOKENS, D), jnp.float32)
        for source in range(target_layer + 1):
            pair = target_layer * (target_layer + 1) // 2 + source
            total = total + jnp.dot(latents[source], dec_weight[pair], preferred_element_type=jnp.float32)
        recons.append(total)
    recon = jnp.stack(recons)
    residual = jnp.stack(targets) - recon
    return recon, residual
```

```python
import jax
import jax.numpy as jnp
from jax import lax
from jax.sharding import Mesh, PartitionSpec as P

BF16 = jnp.bfloat16
F32 = jnp.float32
ROWS = ("zh", "core")
PLANE = ("x", "y")
LAYERS = 3


def exchange(pieces, axis):
    return lax.all_to_all(pieces, axis, split_axis=0, concat_axis=0, tiled=True)


def from_everyone(shard, axis):
    count = lax.axis_size(axis)
    return exchange(jnp.broadcast_to(shard, (count, *shard.shape)), axis)


def body(inputs, gate_up, down_weight, enc_weight, enc_bias, dec_weight):
    layers, rows, width = inputs.shape
    hidden = gate_up.shape[3]
    model = gate_up.shape[1]
    mine = jnp.swapaxes(inputs, 1, 2)
    run = from_everyone(mine, "zl")
    run = jnp.moveaxis(run, 0, 1).reshape(layers, 4 * width, rows)
    everything = from_everyone(run, PLANE)
    features = jnp.moveaxis(everything, 0, 1).reshape(layers, model, rows)

    latents = []
    for layer in range(layers):
        pre = jnp.einsum("dk,dn->kn", enc_weight[layer], features[layer], preferred_element_type=F32)
        latents.append(jax.nn.relu(pre + enc_bias[layer][:, None]).astype(BF16))
    gathered = lax.all_gather(jnp.stack(latents), ROWS, axis=0)

    joined = jnp.transpose(gate_up, (0, 2, 3, 1)).reshape(layers, 2 * hidden, model)
    sums = []
    for layer in range(layers):
        pre = jnp.einsum("jd,dn->jn", joined[layer], features[layer], preferred_element_type=F32)
        act = (jax.nn.gelu(pre[:hidden], approximate=True) * pre[hidden:]).astype(BF16)
        out = jnp.einsum("kf,kn->fn", down_weight[layer], act, preferred_element_type=F32)
        sums.append(out.astype(BF16))
    decoder = jnp.swapaxes(dec_weight, 1, 2)
    for target in range(layers):
        total = None
        for source in range(target + 1):
            pair = target * (target + 1) // 2 + source
            term = jnp.einsum("fk,rkn->rfn", decoder[pair], gathered[:, source], preferred_element_type=F32)
            total = term if total is None else total + term
        sums.append(total.reshape(model, rows).astype(BF16))
    pieces = jnp.stack(sums).reshape(2 * layers, 16, 4 * width, rows)
    arrived = exchange(jnp.moveaxis(pieces, 1, 0), PLANE)
    partial = arrived.astype(F32).sum(axis=0)
    partial = jnp.moveaxis(partial.reshape(2 * layers, 4, width, rows), 1, 0)
    owned = exchange(partial, "zl").sum(axis=0)
    swap = []
    for row in range(4):
        for place in range(4):
            swap.append((row * 4 + place, place * 4 + row))
    recon = lax.ppermute(owned[layers:], ("zh", "core", "x"), swap)
    residual = owned[:layers] - recon
    return jnp.swapaxes(recon, 1, 2), jnp.swapaxes(residual, 1, 2)


def solution(mesh):
    fine = Mesh(mesh.devices.reshape(2, 2, 4, 4, 4), ("zh", "core", "x", "y", "zl"))
    mp = ("x", "y", "zl")
    in_specs = (
        P(None, ROWS, mp),
        P(None, None, None, mp),
        P(None, mp, None),
        P(None, None, mp),
        P(None, mp),
        P(None, mp, ROWS),
    )
    out_specs = (P(None, ROWS, mp), P(None, ROWS, mp))
    return jax.shard_map(body, mesh=fine, in_specs=in_specs, out_specs=out_specs, check_vma=False)
```

```python
import jax
import jax.numpy as jnp
from jax import lax
from jax.sharding import Mesh, PartitionSpec as P

BF16 = jnp.bfloat16
F32 = jnp.float32
ROWS = ("zh", "core")
PLANE = ("x", "y")
LAYERS = 3


def exchange(pieces, axis):
    return lax.all_to_all(pieces, axis, split_axis=0, concat_axis=0, tiled=True)


def from_everyone(shard, axis):
    count = lax.axis_size(axis)
    return exchange(jnp.broadcast_to(shard, (count, *shard.shape)), axis)


def plane_exchange(parts, width):
    layers, model, rows = parts.shape
    return exchange(jnp.moveaxis(parts.reshape(layers, 16, 4 * width, rows), 1, 0), PLANE)


def plane_sum(arrived, width):
    layers, rows = arrived.shape[1], arrived.shape[3]
    partial = arrived.astype(F32).sum(axis=0)
    return jnp.moveaxis(partial.reshape(layers, 4, width, rows), 1, 0)


def permuted_sum(pieces, axis):
    here = lax.axis_index(axis)
    count = pieces.shape[0]
    total = lax.dynamic_index_in_dim(pieces, here, 0, False)
    for step in range(1, count):
        ring = [(index, (index + step) % count) for index in range(count)]
        piece = lax.dynamic_index_in_dim(pieces, (here + step) % count, 0, False)
        total = total + lax.ppermute(piece, axis, ring)
    return total


def body(inputs, gate_up, down_weight, enc_weight, enc_bias, dec_weight):
    layers, rows, width = inputs.shape
    hidden = gate_up.shape[3]
    model = gate_up.shape[1]
    mine = jnp.swapaxes(inputs, 1, 2)
    run = from_everyone(mine, "zl")
    run = jnp.moveaxis(run, 0, 1).reshape(layers, 4 * width, rows)
    everything = from_everyone(run, PLANE)
    features = jnp.moveaxis(everything, 0, 1).reshape(layers, model, rows)

    latents = []
    for layer in range(layers):
        pre = jnp.einsum("dk,dn->kn", enc_weight[layer], features[layer], preferred_element_type=F32)
        latents.append(jax.nn.relu(pre + enc_bias[layer][:, None]).astype(BF16))
    gathered = lax.all_gather(jnp.stack(latents), ROWS, axis=0)

    joined = jnp.transpose(gate_up, (0, 2, 3, 1)).reshape(layers, 2 * hidden, model)
    targets = []
    for layer in range(layers):
        pre = jnp.einsum("jd,dn->jn", joined[layer], features[layer], preferred_element_type=F32)
        act = (jax.nn.gelu(pre[:hidden], approximate=True) * pre[hidden:]).astype(BF16)
        out = jnp.einsum("kf,kn->fn", down_weight[layer], act, preferred_element_type=F32)
        targets.append(out.astype(BF16))
    recons = []
    decoder = jnp.swapaxes(dec_weight, 1, 2)
    for target in range(layers):
        total = None
        for source in range(target + 1):
            pair = target * (target + 1) // 2 + source
            term = jnp.einsum("fk,rkn->rfn", decoder[pair], gathered[:, source], preferred_element_type=F32)
            total = term if total is None else total + term
        recons.append(total.reshape(model, rows).astype(BF16))
    first = plane_exchange(jnp.stack(recons), width)
    outs, first = lax.optimization_barrier((jnp.stack(targets), first))
    second = plane_exchange(outs, width)
    recon = permuted_sum(plane_sum(first, width), "zl")
    swap = []
    for row in range(4):
        for place in range(4):
            swap.append((row * 4 + place, place * 4 + row))
    recon = lax.ppermute(recon, ("zh", "core", "x"), swap)
    second, recon = lax.optimization_barrier((second, recon))
    target = exchange(plane_sum(second, width), "zl").sum(axis=0)
    residual = target - recon
    return jnp.swapaxes(recon, 1, 2), jnp.swapaxes(residual, 1, 2)


def solution(mesh):
    fine = Mesh(mesh.devices.reshape(2, 2, 4, 4, 4), ("zh", "core", "x", "y", "zl"))
    mp = ("x", "y", "zl")
    in_specs = (
        P(None, ROWS, mp),
        P(None, None, None, mp),
        P(None, mp, None),
        P(None, None, mp),
        P(None, mp),
        P(None, mp, ROWS),
    )
    out_specs = (P(None, ROWS, mp), P(None, ROWS, mp))
    return jax.shard_map(body, mesh=fine, in_specs=in_specs, out_specs=out_specs, check_vma=False)
```

```python
import jax
import jax.numpy as jnp
from jax import lax
from jax.experimental import pallas as pl
from jax.experimental.pallas import tpu as pltpu
from jax.sharding import Mesh, PartitionSpec as P

BF16 = jnp.bfloat16
F32 = jnp.float32
ROWS = ("zh", "core")
PLANE = ("x", "y")
LAYERS = 3


def exchange(pieces, axis):
    return lax.all_to_all(pieces, axis, split_axis=0, concat_axis=0, tiled=True)


def from_everyone(shard, axis):
    count = lax.axis_size(axis)
    return exchange(jnp.broadcast_to(shard, (count, *shard.shape)), axis)


STEPS = (1, 3, 2)


def taken(array, index, dim):
    return lax.dynamic_index_in_dim(array, index, dim, False)


def passed_on(array, axis, step):
    count = lax.axis_size(axis)
    return lax.ppermute(array, axis, [(index, (index + step) % count) for index in range(count)])


def stepped(array, axis, step):
    count = lax.axis_size(axis)
    pairs = []
    for core in range(2):
        for index in range(count):
            pairs.append((core * count + index, core * count + (index + (step, count - step)[core]) % count))
    return lax.ppermute(array, ("core", axis), pairs)


def permuted_sums(arrays, axes, dims):
    places = [lax.axis_index(axis) for axis in axes]
    totals = [taken(array, place, dim).astype(F32) for array, place, dim in zip(arrays, places, dims)]
    for step in STEPS:
        for which, (array, axis, place, dim) in enumerate(zip(arrays, axes, places, dims)):
            count = array.shape[dim]
            onward = jnp.where(lax.axis_index("core") == 0, place + step, place + count - step) % count
            piece = stepped(taken(array, onward, dim), axis, step)
            totals[which] = totals[which] + piece.astype(F32)
    return totals


def encode_kernel(features, weight, bias, latent):
    layers, model, _ = weight.shape
    rows = features.shape[3]
    for layer in range(layers):
        rows_in = features[:, layer].reshape(model, rows)
        pre = lax.dot_general(rows_in, weight[layer], (((0,), (0,)), ((), ())), preferred_element_type=F32)
        latent[layer] = jnp.maximum(pre + bias[layer : layer + 1], 0.0).astype(BF16)


def encode(features, weight, bias):
    blocks, layers, deep, rows = features.shape
    _, model, wide = weight.shape
    return pl.pallas_call(
        encode_kernel,
        in_specs=[pl.BlockSpec(memory_space=pltpu.VMEM)] * 3,
        out_specs=pl.BlockSpec(memory_space=pltpu.VMEM),
        out_shape=jax.ShapeDtypeStruct((layers, rows, wide), BF16),
        cost_estimate=pl.CostEstimate(
            flops=2 * layers * model * wide * rows, bytes_accessed=2 * layers * model * (wide + rows), transcendentals=0
        ),
        name="encode",
    )(features, weight, bias)


def mlp_kernel(features, joined, down, out):
    layers, _, hidden, model = joined.shape
    rows = features.shape[3]
    for layer in range(layers):
        rows_in = features[:, layer].reshape(model, rows)
        pre = jnp.dot(joined[layer].reshape(2 * hidden, model), rows_in, preferred_element_type=F32)
        gate = pre[:hidden]
        cubic = gate + 0.044715 * (gate * gate * gate)
        act = 0.5 * gate * (1.0 + jnp.tanh(0.7978845608028654 * cubic)) * pre[hidden:]
        total = lax.dot_general(down[layer], act.astype(BF16), (((0,), (0,)), ((), ())), preferred_element_type=F32)
        out[layer] = total.reshape(out.shape[1:]).astype(BF16)


def mlp(features, joined, down):
    blocks, layers, deep, rows = features.shape
    _, _, hidden, model = joined.shape
    return pl.pallas_call(
        mlp_kernel,
        in_specs=[pl.BlockSpec(memory_space=pltpu.VMEM)] * 3,
        out_specs=pl.BlockSpec(memory_space=pltpu.VMEM),
        out_shape=jax.ShapeDtypeStruct((layers, blocks, deep, rows), BF16),
        cost_estimate=pl.CostEstimate(
            flops=6 * layers * model * hidden * rows,
            bytes_accessed=2 * layers * model * (3 * hidden + 2 * rows),
            transcendentals=layers * hidden * rows,
        ),
        name="mlp",
    )(features, joined, down)


def body(inputs, gate_up, down_weight, enc_weight, enc_bias, dec_weight):
    layers, rows, width = inputs.shape
    hidden = gate_up.shape[3]
    model = gate_up.shape[1]
    mine = jnp.swapaxes(inputs, 1, 2)
    decoder = jnp.swapaxes(dec_weight, 1, 2)
    beside = passed_on(decoder, "core", 1)
    second = lax.axis_index("core") == 1
    decoder = jnp.stack([jnp.where(second, beside, decoder), jnp.where(second, decoder, beside)])
    run = from_everyone(mine, "zl")
    run = jnp.moveaxis(run, 0, 1).reshape(layers, 4 * width, rows)
    everything = from_everyone(run, PLANE)
    everything, decoder = lax.optimization_barrier((everything, decoder))
    own = encode(everything, enc_weight, enc_bias)
    other = passed_on(own, "zh", 1)
    upper = lax.axis_index("zh") == 1
    both = jnp.stack([jnp.where(upper, other, own), jnp.where(upper, own, other)])

    everything, own = lax.optimization_barrier((everything, own))
    outs = mlp(everything, jnp.transpose(gate_up, (0, 2, 3, 1)), down_weight)
    recons = []
    for target in range(layers):
        total = None
        for source in range(target + 1):
            pair = target * (target + 1) // 2 + source
            term = jnp.einsum("cfk,rnk->rcfn", decoder[:, pair], both[:, source], preferred_element_type=F32)
            total = term if total is None else total + term
        recons.append(total.reshape(model, rows).astype(BF16))
    first = jnp.concatenate([jnp.stack(recons).reshape(outs.shape), outs]).reshape(2 * layers, 4, 4, 4 * width, rows)
    cut = 2 * width
    halves = permuted_sums([first[..., :cut, :], first[..., cut:, :]], ["x", "y"], [1, 2])
    halves = permuted_sums([half.astype(BF16) for half in halves], ["y", "x"], [1, 1])
    joint = jnp.concatenate(halves, axis=1).reshape(2 * layers, 4, width, rows)
    joint = permuted_sums([joint], ["zl"], [1])[0]
    summed = joint[:layers]
    swap = []
    for half in range(2):
        for place in range(4):
            swap.append((half * 4 + place, place // 2 * 4 + half * 2 + place % 2))
    recon = lax.ppermute(summed, ("zh", "x"), swap)
    residual = joint[layers:] - recon
    return jnp.swapaxes(recon, 1, 2), jnp.swapaxes(residual, 1, 2)


def solution(mesh):
    fine = Mesh(mesh.devices.reshape(2, 2, 4, 4, 4), ("zh", "core", "x", "y", "zl"))
    mp = ("x", "y", "zl")
    in_specs = (
        P(None, ROWS, mp),
        P(None, None, None, mp),
        P(None, mp, None),
        P(None, None, mp),
        P(None, mp),
        P(None, mp, ROWS),
    )
    out_specs = (P(None, ROWS, mp), P(None, ROWS, mp))
    return jax.shard_map(body, mesh=fine, in_specs=in_specs, out_specs=out_specs, check_vma=False)
```

```python
import jax
import jax.numpy as jnp
from jax import lax
from jax.experimental import pallas as pl
from jax.experimental.pallas import tpu as pltpu
from jax.sharding import Mesh, PartitionSpec as P

BF16 = jnp.bfloat16
F32 = jnp.float32
ROWS = ("zh", "core")
PLANE = ("x", "y")
LAYERS = 3


def exchange(pieces, axis):
    return lax.all_to_all(pieces, axis, split_axis=0, concat_axis=0, tiled=True)


def from_everyone(shard, axis):
    count = lax.axis_size(axis)
    return exchange(jnp.broadcast_to(shard, (count, *shard.shape)), axis)


STEPS = (1, 3, 2)


def taken(array, index, dim):
    return lax.dynamic_index_in_dim(array, index, dim, False)


def passed_on(array, axis, step):
    count = lax.axis_size(axis)
    return lax.ppermute(array, axis, [(index, (index + step) % count) for index in range(count)])


def stepped(array, axis, step):
    count = lax.axis_size(axis)
    pairs = []
    for core in range(2):
        for index in range(count):
            pairs.append((core * count + index, core * count + (index + (step, count - step)[core]) % count))
    return lax.ppermute(array, ("core", axis), pairs)


def permuted_sums(arrays, axes, dims):
    places = [lax.axis_index(axis) for axis in axes]
    totals = [taken(array, place, dim).astype(F32) for array, place, dim in zip(arrays, places, dims)]
    for step in STEPS:
        for which, (array, axis, place, dim) in enumerate(zip(arrays, axes, places, dims)):
            count = array.shape[dim]
            onward = jnp.where(lax.axis_index("core") == 0, place + step, place + count - step) % count
            piece = stepped(taken(array, onward, dim), axis, step)
            totals[which] = totals[which] + piece.astype(F32)
    return totals


def fetch_kernel(source, kept, arrived):
    copy = pltpu.make_async_copy(source, kept, arrived)
    copy.start()
    copy.wait()


def fetch(weight):
    return pl.pallas_call(
        fetch_kernel,
        in_specs=[pl.BlockSpec(memory_space=pl.ANY)],
        out_specs=pl.BlockSpec(memory_space=pltpu.VMEM),
        out_shape=jax.ShapeDtypeStruct(weight.shape, weight.dtype),
        scratch_shapes=[pltpu.SemaphoreType.DMA],
        cost_estimate=pl.CostEstimate(flops=0, bytes_accessed=4 * weight.size, transcendentals=0),
        compiler_params=pltpu.CompilerParams(vmem_limit_bytes=6 << 20),
        name="fetch",
    )(weight)


def encode_kernel(features, weight, bias, latent):
    layers, model, _ = weight.shape
    rows = features.shape[3]
    for layer in range(layers):
        rows_in = features[:, layer].reshape(model, rows)
        pre = lax.dot_general(rows_in, weight[layer], (((0,), (0,)), ((), ())), preferred_element_type=F32)
        latent[layer] = jnp.maximum(pre + bias[layer : layer + 1], 0.0).astype(BF16)


def encode(features, weight, bias):
    blocks, layers, deep, rows = features.shape
    _, model, wide = weight.shape
    return pl.pallas_call(
        encode_kernel,
        in_specs=[pl.BlockSpec(memory_space=pltpu.VMEM)] * 3,
        out_specs=pl.BlockSpec(memory_space=pltpu.VMEM),
        out_shape=jax.ShapeDtypeStruct((layers, rows, wide), BF16),
        cost_estimate=pl.CostEstimate(
            flops=2 * layers * model * wide * rows, bytes_accessed=2 * layers * model * (wide + rows), transcendentals=0
        ),
        compiler_params=pltpu.CompilerParams(vmem_limit_bytes=8 << 20),
        name="encode",
    )(features, weight, bias)


def mlp_kernel(features, joined, down, out):
    layers, _, hidden, model = joined.shape
    rows = features.shape[3]
    for layer in range(layers):
        rows_in = features[:, layer].reshape(model, rows)
        pre = jnp.dot(joined[layer].reshape(2 * hidden, model), rows_in, preferred_element_type=F32)
        gate = pre[:hidden]
        cubic = gate + 0.044715 * (gate * gate * gate)
        act = 0.5 * gate * (1.0 + jnp.tanh(0.7978845608028654 * cubic)) * pre[hidden:]
        total = lax.dot_general(down[layer], act.astype(BF16), (((0,), (0,)), ((), ())), preferred_element_type=F32)
        out[layer] = total.reshape(out.shape[1:]).astype(BF16)


def mlp(features, joined, down):
    blocks, layers, deep, rows = features.shape
    _, _, hidden, model = joined.shape
    return pl.pallas_call(
        mlp_kernel,
        in_specs=[pl.BlockSpec(memory_space=pltpu.VMEM)] * 3,
        out_specs=pl.BlockSpec(memory_space=pltpu.VMEM),
        out_shape=jax.ShapeDtypeStruct((layers, blocks, deep, rows), BF16),
        cost_estimate=pl.CostEstimate(
            flops=6 * layers * model * hidden * rows,
            bytes_accessed=2 * layers * model * (3 * hidden + 2 * rows),
            transcendentals=layers * hidden * rows,
        ),
        compiler_params=pltpu.CompilerParams(vmem_limit_bytes=16 << 20),
        name="mlp",
    )(features, joined, down)


def body(inputs, gate_up, down_weight, enc_weight, enc_bias, dec_weight):
    layers, rows, width = inputs.shape
    hidden = gate_up.shape[3]
    model = gate_up.shape[1]
    mine = jnp.swapaxes(inputs, 1, 2)
    decoder = jnp.swapaxes(dec_weight, 1, 2)
    beside = passed_on(decoder, "core", 1)
    second = lax.axis_index("core") == 1
    decoder = jnp.stack([jnp.where(second, beside, decoder), jnp.where(second, decoder, beside)])
    run = from_everyone(mine, "zl")
    run = jnp.moveaxis(run, 0, 1).reshape(layers, 4 * width, rows)
    everything = from_everyone(run, PLANE)
    everything, decoder, encoder = lax.optimization_barrier((everything, decoder, fetch(enc_weight)))
    own = encode(everything, encoder, enc_bias)
    other = passed_on(own, "zh", 1)
    upper = lax.axis_index("zh") == 1
    both = jnp.stack([jnp.where(upper, other, own), jnp.where(upper, own, other)])

    everything, own = lax.optimization_barrier((everything, own))
    outs = mlp(everything, jnp.transpose(gate_up, (0, 2, 3, 1)), down_weight)
    recons = []
    for target in range(layers):
        total = None
        for source in range(target + 1):
            pair = target * (target + 1) // 2 + source
            term = jnp.einsum("cfk,rnk->rcfn", decoder[:, pair], both[:, source], preferred_element_type=F32)
            total = term if total is None else total + term
        recons.append(total.reshape(model, rows).astype(BF16))
    first = jnp.concatenate([jnp.stack(recons).reshape(outs.shape), outs]).reshape(2 * layers, 4, 4, 4 * width, rows)
    cut = 2 * width
    halves = permuted_sums([first[..., :cut, :], first[..., cut:, :]], ["x", "y"], [1, 2])
    halves = permuted_sums([half.astype(BF16) for half in halves], ["y", "x"], [1, 1])
    joint = jnp.concatenate(halves, axis=1).reshape(2 * layers, 4, width, rows)
    joint = permuted_sums([joint], ["zl"], [1])[0]
    summed = joint[:layers]
    swap = []
    for half in range(2):
        for place in range(4):
            swap.append((half * 4 + place, place // 2 * 4 + half * 2 + place % 2))
    recon = lax.ppermute(summed, ("zh", "x"), swap)
    residual = joint[layers:] - recon
    return jnp.swapaxes(recon, 1, 2), jnp.swapaxes(residual, 1, 2)


def solution(mesh):
    fine = Mesh(mesh.devices.reshape(2, 2, 4, 4, 4), ("zh", "core", "x", "y", "zl"))
    mp = ("x", "y", "zl")
    in_specs = (
        P(None, ROWS, mp),
        P(None, None, None, mp),
        P(None, mp, None),
        P(None, None, mp),
        P(None, mp),
        P(None, mp, ROWS),
    )
    out_specs = (P(None, ROWS, mp), P(None, ROWS, mp))
    return jax.shard_map(body, mesh=fine, in_specs=in_specs, out_specs=out_specs, check_vma=False)
```
